32 devices in a mesh: op: 4 (over z), sec: 8 (over y, x, core).
Axes of the slice: x: 2, y: 2, z: 4, core: 2. Of those that a mesh axis runs over, the one named last changes fastest.
Arguments:
- state_vector: bfloat16 [512, 8, 512], P(None, 'sec'), may hold values from -6 to 6
- left_env: bfloat16 [60, 8, 512, 512], P('op', 'sec'), may hold values from -0.25 to 0.25
- right_env: bfloat16 [60, 8, 512, 512], P('op', 'sec'), may hold values from -0.03125 to 0.03125
- op_shift: int32 [60, 2], P('op'), may hold values from -1 to 1, as said below
- sector_charge: int32 [8, 2], replicated, may hold values from 0 to 3, as said below
Outputs:
- hpsi: bfloat16 [512, 8, 512], P('op', 'sec')
The draws below stay inside these ranges and needn't reach their ends.
Inputs may be any that keep to these rules, and one draw needn't show every extreme that they name: `sector_charge`: row n holds the charges of the sector in slot n; the rows are the 2 x 4 pairs (up below 2, down below 4), each once. `op_shift`: each operator changes at most one of the two charges.
All inputs are finite; a program needn't handle non-finite values.
Results may differ from the reference program's by a relative error of at most 0.0049.
Values may be sent and summed in bfloat16 or wider, within the bound.
No kernel may reach another device: no remote copies, remote signals or barrier semaphores. Data moves between devices by JAX's collectives and lax.ppermute only.
A program may use at most 128 MiB of HBM per device.

```python
import jax
import jax.numpy as jnp
from jax import lax

K = 512
OPS = 60
NSEC = 8
QDN = 4


def draw_sector_charge(key, part):
    order = jax.random.permutation(key, NSEC)
    return jnp.stack([order // QDN, order % QDN], axis=1).astype(jnp.int32)


def draw_op_shift(key, part):
    kinds = jax.random.randint(jax.random.fold_in(key, 11), (OPS,), 0, 6).astype(jnp.int32)
    order = jax.random.permutation(jax.random.fold_in(key, 12), OPS)
    kinds = kinds.at[order[:4]].set(jnp.arange(2, 6, dtype=jnp.int32))
    table = jnp.array([[0, 0], [0, 0], [1, 0], [-1, 0], [0, 1], [0, -1]], dtype=jnp.int32)
    return jnp.take(table, kinds, axis=0).astype(jnp.int32)


def levels(rng, dims, cuts, least, largest):
    factor_of, own = 1.0, jax.random.fold_in(rng, 6)
    for dim, shards_of in cuts:
        heights = jnp.exp(jax.random.uniform(jax.random.fold_in(own, dim), (shards_of,), jnp.float32, least / len(cuts), largest / len(cuts)))
        factor_of = factor_of * jnp.repeat(heights, dims[dim] // shards_of).reshape([-1 if axis == dim else 1 for axis in range(len(dims))])
    return factor_of


def centred(stream_key, dims, scale, reach, pieces=(), kind=jnp.bfloat16):
    drawn = scale * jax.random.normal(stream_key, dims, jnp.float32)
    if pieces:
        drawn = drawn * levels(stream_key, dims, pieces, -0.22, 0.18)
    return jnp.clip(drawn, -reach, reach).astype(kind)


def setup_inputs(seed: int = 0) -> dict:
    key_of = jax.random.split(jax.random.key(seed), 6)
    return {
        "state_vector": centred(key_of[0], (K, NSEC, K), 1.0, 6.0, ((1, 8),)),
        "left_env": centred(key_of[1], (OPS, NSEC, K, K), K ** -0.5, 0.25, ((0, 4), (1, 8))),
        "right_env": centred(key_of[2], (OPS, NSEC, K, K), (K * OPS) ** -0.5, 0.03125, ((0, 4), (1, 8))),
        "op_shift": draw_op_shift(jax.random.fold_in(key_of[5], 71), 0),
        "sector_charge": draw_sector_charge(jax.random.fold_in(key_of[5], 71), 0),
    }


def find_sources(own_charge, all_charge, op_shift):
    target = own_charge[None, :, :] - op_shift[:, None, :]
    matches = jnp.all(target[:, :, None, :] == all_charge[None, None, :, :], axis=-1)
    slot_ids = jnp.arange(all_charge.shape[0], dtype=jnp.int32)
    source_slot = jnp.sum(jnp.where(matches, slot_ids, 0), axis=-1).astype(jnp.int32)
    present = jnp.any(matches, axis=-1)
    return source_slot, present


def reference(state_vector, left_env, right_env, op_shift, sector_charge):
    source_slot, present = find_sources(sector_charge, sector_charge, op_shift)

    def apply_slot(slot_index):
        sources = jnp.take(state_vector, source_slot[:, slot_index], axis=1)
        sources = jnp.where(present[:, slot_index][None, :, None], sources, jnp.zeros((), sources.dtype))
        left_block = left_env[:, slot_index].astype(jnp.float32)
        halfway = jnp.einsum('bij,jbk->bik', left_block, sources.astype(jnp.float32)).astype(jnp.bfloat16)
        right_block = right_env[:, slot_index].astype(jnp.float32)
        summed = jnp.einsum('bik,blk->il', halfway.astype(jnp.float32), right_block)
        return summed.astype(jnp.bfloat16)

    result = lax.map(apply_slot, jnp.arange(NSEC, dtype=jnp.int32))
    return jnp.transpose(result, (1, 0, 2))
```

```python
import functools

import jax
import jax.numpy as jnp
from jax import lax
from jax.experimental import pallas as pl
from jax.experimental.pallas import tpu as pltpu
from jax.sharding import PartitionSpec as P

SIDE = 6
SMEM = pl.BlockSpec(memory_space=pltpu.SMEM)
VMEM = pl.BlockSpec(memory_space=pltpu.VMEM)
HBM = pl.BlockSpec(memory_space=pltpu.HBM)
ANY = pl.BlockSpec(memory_space=pl.ANY)


def fill_table(charge, table):
    for i in range(SIDE * SIDE):
        table[i] = -1
    for n in range(charge.shape[1]):
        table[(charge[0, n] + 1) * SIDE + charge[1, n] + 1] = n


def list_operators(me, position_of, shift, charge, table, order, low, high):
    base = (charge[0, me] + 1) * SIDE + charge[1, me] + 1

    def visit(b, count):
        slot = table[base - shift[0, b] * SIDE - shift[1, b]]
        position = position_of(me, slot)
        order[0, count] = b
        order[1, count] = position - low
        here = (slot >= 0) & (position >= low) & (position < high)
        return count + here.astype(jnp.int32)

    return lax.fori_loop(0, shift.shape[1], visit, jnp.int32(0))


def add_product(total, left, source, right):
    halfway = jnp.dot(left, source, preferred_element_type=jnp.float32).astype(jnp.bfloat16)
    total[...] += lax.dot_general(
        halfway, right, (((1,), (1,)), ((), ())), preferred_element_type=jnp.float32
    )


def load_sources(pieces, refs, source, sems):
    copies = []
    for i, sizes in enumerate(pieces):
        begin = 0
        for size in sizes:
            at = len(copies)
            copies.append(
                pltpu.make_async_copy(refs[at], source.at[i, pl.ds(begin, size)], sems.at[at])
            )
            begin += size
    for copy in copies:
        copy.start()
    return copies


def store(last, ops, total, outs):
    if not last:
        outs[0][...] = total[...]
        return
    rows = total.shape[0] // ops
    mine = lax.axis_index("op")
    for j in range(ops):
        begin = pl.multiple_of((mine ^ j) * rows, rows)
        outs[j][...] = total[pl.ds(begin, rows), :].astype(outs[j].dtype)


def first_kernel(pieces, position_of, slots, last, ops, *refs):
    shift, charge, left_hbm, right_hbm = refs[:4]
    n_in = sum(len(p) for p in pieces)
    inputs, rest = refs[4 : 4 + n_in], refs[4 + n_in :]
    n_out = ops if last else 1
    outs, rest = rest[:n_out], rest[n_out:]
    left, right, source, total, table, now, later, sems, source_sems = rest
    me = lax.axis_index("sec")
    fill_table(charge, table)
    here = len(pieces)
    count = list_operators(me, position_of, shift, charge, table, now, 0, here)

    def copies(b):
        return (
            pltpu.make_async_copy(left_hbm.at[b], left.at[b], sems.at[0, b]),
            pltpu.make_async_copy(right_hbm.at[b], right.at[b], sems.at[1, b]),
        )

    def start(order):
        def body(i, carry):
            for copy in copies(order[0, i]):
                copy.start()
            return carry

        return body

    def wait(order):
        def body(i, carry):
            for copy in copies(order[0, i]):
                copy.wait()
            return carry

        return body

    loads = load_sources(pieces, inputs, source, source_sems)
    lax.fori_loop(0, count, start(now), 0)
    if here < slots:
        others = list_operators(me, position_of, shift, charge, table, later, here, slots)
        lax.fori_loop(0, others, start(later), 0)
    total[...] = jnp.zeros_like(total)
    for load in loads:
        load.wait()

    def body(i, carry):
        b = now[0, i]
        for copy in copies(b):
            copy.wait()
        add_product(total, left[b], source[now[1, i]], right[b])
        return carry

    lax.fori_loop(0, count, body, 0)
    if here < slots:
        lax.fori_loop(0, others, wait(later), 0)
    store(last, ops, total, outs)


def next_kernel(pieces, low, position_of, last, ops, *refs):
    shift, charge, left, right, before = refs[:5]
    n_in = sum(len(p) for p in pieces)
    inputs, rest = refs[5 : 5 + n_in], refs[5 + n_in :]
    n_out = ops if last else 1
    outs, (source, total, table, order, source_sems) = rest[:n_out], rest[n_out:]
    me = lax.axis_index("sec")
    loads = load_sources(pieces, inputs, source, source_sems)
    total[...] = before[...]
    fill_table(charge, table)
    count = list_operators(me, position_of, shift, charge, table, order, low, low + len(pieces))
    for load in loads:
        load.wait()

    def body(i, carry):
        b = order[0, i]
        add_product(total, left[b], source[order[1, i]], right[b])
        return carry

    lax.fori_loop(0, count, body, 0)
    store(last, ops, total, outs)


def run(blocks, low, position_of, slots, shift, charge, left_env, right_env, before, last, ops):
    pieces = [[p.shape[0] for p in block] for block in blocks]
    flat = [p for block in blocks for p in block]
    operators, rows, inner = left_env.shape
    columns, width = right_env.shape[1:]
    if last:
        out_shape = [
            jax.ShapeDtypeStruct((rows // ops, columns), jnp.float32 if j == 0 else jnp.bfloat16)
            for j in range(ops)
        ]
    else:
        out_shape = [jax.ShapeDtypeStruct((rows, columns), jnp.float32)]
    scratch = [
        pltpu.VMEM((len(blocks), inner, width), jnp.bfloat16),
        pltpu.VMEM((rows, columns), jnp.float32),
        pltpu.SMEM((SIDE * SIDE,), jnp.int32),
        pltpu.SMEM((2, operators + 1), jnp.int32),
    ]
    source_sems = pltpu.SemaphoreType.DMA((len(flat),))
    if before is None:
        kernel = functools.partial(first_kernel, pieces, position_of, slots, last, ops)
        out_shape += [
            jax.ShapeDtypeStruct(left_env.shape, left_env.dtype),
            jax.ShapeDtypeStruct(right_env.shape, right_env.dtype),
        ]
        scratch += [
            pltpu.SMEM((2, operators + 1), jnp.int32),
            pltpu.SemaphoreType.DMA((2, operators)),
        ]
        in_specs = [SMEM, SMEM, HBM, HBM]
        extra = ()
    else:
        kernel = functools.partial(next_kernel, pieces, low, position_of, last, ops)
        in_specs = [SMEM, SMEM, VMEM, VMEM, VMEM]
        extra = (before,)
    share = max(1, operators * len(blocks) // slots)
    return pl.pallas_call(
        kernel,
        out_shape=out_shape,
        in_specs=in_specs + [ANY] * len(flat),
        out_specs=[VMEM] * len(out_shape),
        scratch_shapes=scratch + [source_sems],
        compiler_params=pltpu.CompilerParams(vmem_limit_bytes=32 << 20),
        cost_estimate=pl.CostEstimate(
            flops=share * 4 * rows * inner * width,
            bytes_accessed=share * 4 * rows * inner,
            transcendentals=0,
        ),
    )(shift, charge, left_env, right_env, *extra, *flat)


def send(a, axis, size, flip):
    return lax.ppermute(a, axis, [(i, i ^ flip) for i in range(size)])


def by_flip(me, slot):
    return slot ^ me


def by_slot(me, slot):
    return slot


def on_device(secs, ops, state_vector, left_env, right_env, op_shift, sector_charge):
    own = state_vector.reshape(state_vector.shape[0], state_vector.shape[2])
    left_env = left_env.reshape(left_env.shape[0], *left_env.shape[2:])
    right_env = right_env.reshape(right_env.shape[0], *right_env.shape[2:])
    add = functools.partial(
        run, slots=secs, shift=op_shift.T, charge=sector_charge.T, ops=ops
    )
    if secs == 8:
        half = own.shape[0] // 2
        flip = functools.partial(send, axis="sec", size=secs)
        across_x, across_y, sibling = flip(own, flip=2), flip(own, flip=4), flip(own, flip=1)
        total, left, right = add(
            [[own], [sibling]], 0, by_flip, left_env=left_env, right_env=right_env,
            before=None, last=False,
        )
        across_x, across_y, total = lax.optimization_barrier((across_x, across_y, total))
        far_top = flip(across_y[:half], flip=2)
        far_bottom = flip(across_x[half:], flip=4)
        across_x_sibling, across_y_sibling = flip(across_x, flip=1), flip(across_y, flip=1)
        (total,) = add(
            [[across_x], [across_x_sibling], [across_y], [across_y_sibling]],
            2, by_flip, left_env=left, right_env=right, before=total, last=False,
        )
        far_top, far_bottom, total = lax.optimization_barrier((far_top, far_bottom, total))
        far_top_sibling, far_bottom_sibling = flip(far_top, flip=1), flip(far_bottom, flip=1)
        parts = add(
            [[far_top, far_bottom], [far_top_sibling, far_bottom_sibling]],
            6, by_flip, left_env=left, right_env=right, before=total, last=True,
        )
    else:
        gathered = lax.all_gather(own, "sec", axis=0)
        parts = add(
            [[gathered[n]] for n in range(secs)], 0, by_slot, left_env=left_env,
            right_env=right_env, before=None, last=True,
        )
    return scatter_sum(parts, ops).astype(jnp.bfloat16)[:, None, :]


def scatter_sum(parts, ops):
    result = parts[0]
    for j in range(1, ops):
        result = result + send(parts[j], "op", ops, j).astype(jnp.float32)
    return result


def solution(mesh):
    placed = (
        P(None, "sec", None),
        P("op", "sec", None, None),
        P("op", "sec", None, None),
        P("op", None),
        P(),
    )
    return jax.shard_map(
        functools.partial(on_device, mesh.shape["sec"], mesh.shape["op"]),
        mesh=mesh,
        in_specs=placed,
        out_specs=P("op", "sec", None),
        check_vma=False,
    )
```

```python
import functools

import jax
import jax.numpy as jnp
from jax import lax
from jax.experimental import pallas as pl
from jax.experimental.pallas import tpu as pltpu
from jax.sharding import PartitionSpec as P

SIDE = 6
LIMIT = 6
SMEM = pl.BlockSpec(memory_space=pltpu.SMEM)
VMEM = pl.BlockSpec(memory_space=pltpu.VMEM)
HBM = pl.BlockSpec(memory_space=pltpu.HBM)
ANY = pl.BlockSpec(memory_space=pl.ANY)


def find_positions(me, position_of, shift, charge, table, plan):
    for i in range(SIDE * SIDE):
        table[i] = -1
    for n in range(charge.shape[1]):
        table[(charge[0, n] + 1) * SIDE + charge[1, n] + 1] = n
    base = (charge[0, me] + 1) * SIDE + charge[1, me] + 1

    def visit(b, carry):
        slot = table[base - shift[0, b] * SIDE - shift[1, b]]
        plan[b] = jnp.where(slot < 0, -1, position_of(me, slot))
        return carry

    lax.fori_loop(0, shift.shape[1], visit, 0)


def list_operators(plan, order, places, skip=0):
    def visit(b, carry):
        count, seen = carry
        position = plan[b]
        index = jnp.int32(-1)
        for i, place in enumerate(places):
            index = jnp.where(position == place, i, index)
        order[0, count] = b
        order[1, count] = index
        here = index >= 0
        if skip:
            here = here & ((position != 0) | (seen >= skip))
            seen = seen + (position == 0).astype(jnp.int32)
        return count + here.astype(jnp.int32), seen

    return lax.fori_loop(0, plan.shape[0], visit, (jnp.int32(0), jnp.int32(0)))[0]


def product(left, source, right):
    halfway, begin = None, 0
    for piece in source:
        end = begin + piece.shape[0]
        term = jnp.dot(left[:, begin:end], piece[...], preferred_element_type=jnp.float32)
        halfway, begin = term if halfway is None else halfway + term, end
    halfway = halfway.astype(jnp.bfloat16)
    return lax.dot_general(halfway, right[...], (((1,), (1,)), ((), ())), preferred_element_type=jnp.float32)


def add_operators(total, count, order, left, right, source, ready):
    def term(i):
        b = order[0, i]
        ready(b)
        return left.at[b], source(order[1, i]), right.at[b]

    def pair(i, carry):
        one, two = term(2 * i), term(2 * i + 1)
        total[...] += product(*one) + product(*two)
        return carry

    lax.fori_loop(0, count // 2, pair, 0)

    @pl.when(count % 2 == 1)
    def _():
        total[...] += product(*term(count - 1))


def each(count, order, act, begin=0):
    def body(i, carry):
        act(order[0, i])
        return carry

    lax.fori_loop(begin, count, body, 0)


class Loads:
    def __init__(self, left_hbm, right_hbm, left, right, sems):
        self.refs = left_hbm, right_hbm, left, right, sems

    def both(self, b, at):
        left_hbm, right_hbm, left, right, sems = self.refs
        return (
            pltpu.make_async_copy(left_hbm.at[b], left.at[at], sems.at[0, at]),
            pltpu.make_async_copy(right_hbm.at[b], right.at[at], sems.at[1, at]),
        )

    def start(self, b, at=None):
        for copy in self.both(b, b if at is None else at):
            copy.start()

    def wait(self, b, at=None):
        for copy in self.both(b, b if at is None else at):
            copy.wait()


def load_sources(pieces, refs, source, sems):
    copies = []
    for i, sizes in enumerate(pieces):
        begin = 0
        for size in sizes:
            at = len(copies)
            copies.append(
                pltpu.make_async_copy(refs[at], source.at[i, pl.ds(begin, size)], sems.at[at])
            )
            begin += size
    for copy in copies:
        copy.start()
    return copies


def first_kernel(position_of, limit, shift_hbm, charge_hbm, left_hbm, right_hbm, own_hbm, *refs):
    total, plan, left, right, source, shift, charge, table, order, sems, small = refs
    copies = [
        pltpu.make_async_copy(shift_hbm, shift, small.at[0]),
        pltpu.make_async_copy(charge_hbm, charge, small.at[1]),
        pltpu.make_async_copy(own_hbm, source.at[0], small.at[2]),
    ]
    for copy in copies:
        copy.start()
    for copy in copies[:2]:
        copy.wait()
    find_positions(lax.axis_index("sec"), position_of, shift, charge, table, plan)
    count = jnp.minimum(list_operators(plan, order, [0]), limit)
    loads = Loads(left_hbm, right_hbm, left, right, sems)

    def start(i, carry):
        loads.start(order[0, i], i)
        order[0, i] = i
        return carry

    lax.fori_loop(0, count, start, 0)
    total[...] = jnp.zeros_like(total)
    copies[2].wait()
    add_operators(
        total, count, order, left, right, lambda at: [source.at[at]], lambda at: loads.wait(0, at)
    )


def second_kernel(pieces, places, skip, others, *refs):
    plan, left_hbm, right_hbm = refs[:3]
    n_in = sum(len(p) for p in pieces)
    inputs, rest = refs[4 : 4 + n_in], refs[4 + n_in :]
    total, left, right, source, now, later, sems, source_sems = rest
    loads = Loads(left_hbm, right_hbm, left, right, sems)
    sources = load_sources(pieces, inputs, source, source_sems)
    count = list_operators(plan, now, places, skip)
    each(count, now, loads.start)
    behind = list_operators(plan, later, others)
    each(behind, later, loads.start)
    for copy in sources:
        copy.wait()
    add_operators(total, count, now, left, right, lambda at: [source.at[at]], loads.wait)
    each(behind, later, loads.wait)


def next_kernel(counts, places, sends, plan, left, right, before, *refs):
    del before
    flat = refs[: sum(counts)]
    total, *outs, order = refs[sum(counts) :]
    begin = 0
    for n, place in zip(counts, places):
        block = flat[begin : begin + n]
        begin += n
        count = list_operators(plan, order, [place])
        add_operators(total, count, order, left, right, lambda at: block, lambda b: None)
    for out, flip in zip(outs, sends):
        rows = out.shape[0]
        at = pl.multiple_of((lax.axis_index("op") ^ flip) * rows, rows)
        out[...] = total[pl.ds(at, rows), :].astype(out.dtype)


def general_kernel(slots, *refs):
    shift, charge, left_hbm, right_hbm, blocks_hbm = refs[:5]
    total, source, left, right, plan, table, order, sems, block_sem = refs[5:]
    copy = pltpu.make_async_copy(blocks_hbm, source, block_sem)
    copy.start()
    find_positions(lax.axis_index("sec"), by_slot, shift, charge, table, plan)
    count = list_operators(plan, order, range(slots))
    loads = Loads(left_hbm, right_hbm, left, right, sems)
    each(count, order, loads.start)
    total[...] = jnp.zeros_like(total)
    copy.wait()
    add_operators(total, count, order, left, right, lambda at: [source.at[at]], loads.wait)


def cost(flops, moved):
    return pl.CostEstimate(flops=flops, bytes_accessed=moved, transcendentals=0)


def in_hbm(x):
    return pltpu.with_memory_space_constraint(x, pltpu.HBM)


def limit_vmem(mib):
    return pltpu.CompilerParams(vmem_limit_bytes=mib << 20)


def start_sum(own, position_of, limit, shift, charge, left_env, right_env):
    operators, rows, inner = left_env.shape
    columns, width = right_env.shape[1:]
    return pl.pallas_call(
        functools.partial(first_kernel, position_of, limit),
        out_shape=[
            jax.ShapeDtypeStruct((rows, columns), jnp.float32),
            jax.ShapeDtypeStruct((operators,), jnp.int32),
        ],
        in_specs=[HBM] * 5,
        out_specs=[VMEM, SMEM],
        scratch_shapes=[
            pltpu.VMEM((limit, rows, inner), jnp.bfloat16),
            pltpu.VMEM((limit, columns, width), jnp.bfloat16),
            pltpu.VMEM((1, inner, width), jnp.bfloat16),
            pltpu.SMEM(shift.shape, jnp.int32),
            pltpu.SMEM(charge.shape, jnp.int32),
            pltpu.SMEM((SIDE * SIDE,), jnp.int32),
            pltpu.SMEM((2, operators + 1), jnp.int32),
            pltpu.SemaphoreType.DMA((2, limit)),
            pltpu.SemaphoreType.DMA((3,)),
        ],
        compiler_params=limit_vmem(24),
        cost_estimate=cost(limit * 4 * rows * inner * width, limit * 4 * rows * inner),
    )(in_hbm(shift), in_hbm(charge), in_hbm(left_env), in_hbm(right_env), in_hbm(own))


def add_and_load(blocks, places, skip, others, plan, left_env, right_env, before):
    pieces = [[p.shape[0] for p in block] for block in blocks]
    flat = [p for block in blocks for p in block]
    operators, rows, inner = left_env.shape
    columns, width = right_env.shape[1:]
    return pl.pallas_call(
        functools.partial(second_kernel, pieces, places, skip, others),
        out_shape=[
            jax.ShapeDtypeStruct(before.shape, jnp.float32),
            jax.ShapeDtypeStruct(left_env.shape, left_env.dtype),
            jax.ShapeDtypeStruct(right_env.shape, right_env.dtype),
        ],
        in_specs=[SMEM, HBM, HBM, VMEM] + [ANY] * len(flat),
        out_specs=[VMEM] * 3,
        input_output_aliases={3: 0},
        scratch_shapes=[
            pltpu.VMEM((len(blocks), inner, width), jnp.bfloat16),
            pltpu.SMEM((2, operators + 1), jnp.int32),
            pltpu.SMEM((2, operators + 1), jnp.int32),
            pltpu.SemaphoreType.DMA((2, operators)),
            pltpu.SemaphoreType.DMA((len(flat),)),
        ],
        compiler_params=limit_vmem(24),
        cost_estimate=cost(operators * 2 * rows * inner * width, operators * 4 * rows * inner),
    )(plan, in_hbm(left_env), in_hbm(right_env), before, *flat)


def add_blocks(blocks, places, sends, ops, plan, left, right, before):
    flat = [p for block in blocks for p in block]
    operators, rows, inner = left.shape
    columns, width = right.shape[1:]
    return pl.pallas_call(
        functools.partial(next_kernel, [len(block) for block in blocks], places, sends),
        out_shape=[jax.ShapeDtypeStruct((rows, columns), jnp.float32)]
        + [
            jax.ShapeDtypeStruct((rows // ops, columns), jnp.bfloat16 if flip else jnp.float32)
            for flip in sends
        ],
        in_specs=[SMEM] + [VMEM] * (3 + len(flat)),
        out_specs=[VMEM] * (1 + len(sends)),
        scratch_shapes=[pltpu.SMEM((2, operators + 1), jnp.int32)],
        input_output_aliases={3: 0},
        compiler_params=limit_vmem(16),
        cost_estimate=cost(operators * rows * inner * width, operators * rows * inner),
    )(plan, left, right, before, *flat)


def sum_all(blocks, shift, charge, left_env, right_env):
    operators, rows, inner = left_env.shape
    columns, width = right_env.shape[1:]
    return pl.pallas_call(
        functools.partial(general_kernel, blocks.shape[0]),
        out_shape=jax.ShapeDtypeStruct((rows, columns), jnp.float32),
        in_specs=[SMEM, SMEM] + [HBM] * 3,
        out_specs=VMEM,
        scratch_shapes=[
            pltpu.VMEM(blocks.shape, blocks.dtype),
            pltpu.VMEM(left_env.shape, left_env.dtype),
            pltpu.VMEM(right_env.shape, right_env.dtype),
            pltpu.SMEM((operators,), jnp.int32),
            pltpu.SMEM((SIDE * SIDE,), jnp.int32),
            pltpu.SMEM((2, operators + 1), jnp.int32),
            pltpu.SemaphoreType.DMA((2, operators)),
            pltpu.SemaphoreType.DMA,
        ],
        compiler_params=limit_vmem(48),
        cost_estimate=cost(operators * 4 * rows * inner * width, operators * 4 * rows * inner),
    )(shift, charge, left_env, right_env, blocks)


def by_slot(me, slot):
    return slot


def by_arrival(me, slot):
    flip = slot ^ me
    turned = ((me ^ lax.axis_index("op")) & 1) == 1
    return jnp.where(turned & (flip >= 2) & (flip < 6), flip ^ 6, flip)


def on_eight(ops, op_shift, sector_charge, own, left_env, right_env):
    secs = 8
    axes = ("op", "sec")
    devices = [(z, s) for z in range(ops) for s in range(secs)]

    def pairs(move):
        return [(z * secs + s, (lambda t: t[0] * secs + t[1])(move(z, s))) for z, s in devices]

    first_flip = lambda z, s: 2 if (z + s) % 2 == 0 else 4
    to_first = pairs(lambda z, s: (z, s ^ first_flip(z, s)))
    to_second = pairs(lambda z, s: (z, s ^ 6 ^ first_flip(z, s)))
    to_core = pairs(lambda z, s: (z, s ^ 1))
    to_plane = pairs(lambda z, s: (z ^ 1, s))
    cut = own.shape[0] // 2
    barrier = lax.optimization_barrier
    later = (3, 4, 6, 7)

    first = lax.ppermute(own, axes, to_first)
    second_bottom = lax.ppermute(own[cut:], axes, to_second)
    other = lax.ppermute(own, axes, to_core)
    total, plan = start_sum(
        own, by_arrival, LIMIT, op_shift.T, sector_charge.T, left_env, right_env
    )
    first, total = barrier((first, total))
    second_top = lax.ppermute(first[:cut], axes, to_plane)
    far = lax.ppermute(first, axes, to_second)
    other_first = lax.ppermute(first, axes, to_core)
    total, left, right = add_and_load(
        [[own], [other], [first], [other_first]], (0, 1, 2, 5), LIMIT, later,
        plan, left_env, right_env, total,
    )
    second_bottom, total = barrier((second_bottom, total))
    other_second_bottom = lax.ppermute(second_bottom, axes, to_core)
    add = functools.partial(add_blocks, ops=ops, plan=plan, left=left, right=right)
    second_top, far, total = barrier((second_top, far, total))
    other_second_top = lax.ppermute(second_top, axes, to_core)
    other_far = lax.ppermute(far, axes, to_core)
    (total,) = add([[second_top, second_bottom], [far]], (4, 6), (), before=total)
    _, *parts = add(
        [[other_second_top, other_second_bottom], [other_far]], (3, 7), tuple(range(ops)),
        before=total,
    )
    result = parts[0]
    for flip in (3, 2, 1):
        sent = lax.ppermute(parts[flip], "op", [(i, i ^ flip) for i in range(ops)])
        result = result + sent.astype(jnp.float32)
    return result


def on_any(secs, ops, op_shift, sector_charge, own, left_env, right_env):
    gathered = lax.all_gather(own, "sec", axis=0)
    total = sum_all(gathered, op_shift.T, sector_charge.T, left_env, right_env)
    rows = total.shape[0] // ops
    me = lax.axis_index("op")
    part = lambda flip: lax.dynamic_slice_in_dim(total, (me ^ flip) * rows, rows, 0)
    result = part(0)
    for flip in range(1, ops):
        sent = part(flip).astype(jnp.bfloat16)
        sent = lax.ppermute(sent, "op", [(i, i ^ flip) for i in range(ops)])
        result = result + sent.astype(jnp.float32)
    return result


def on_device(secs, ops, state_vector, left_env, right_env, op_shift, sector_charge):
    own = state_vector.reshape(state_vector.shape[0], state_vector.shape[2])
    left_env = left_env.reshape(left_env.shape[0], *left_env.shape[2:])
    right_env = right_env.reshape(right_env.shape[0], *right_env.shape[2:])
    apply = (
        functools.partial(on_eight, ops)
        if secs == 8 and ops == 4
        else functools.partial(on_any, secs, ops)
    )
    hpsi = apply(op_shift, sector_charge, own, left_env, right_env)
    return hpsi.astype(jnp.bfloat16)[:, None, :]


def solution(mesh):
    placed = (
        P(None, "sec", None),
        P("op", "sec", None, None),
        P("op", "sec", None, None),
        P("op", None),
        P(),
    )
    return jax.shard_map(
        functools.partial(on_device, mesh.shape["sec"], mesh.shape["op"]),
        mesh=mesh,
        in_specs=placed,
        out_specs=P("op", "sec", None),
        check_vma=False,
    )
```

```python
import functools

import jax
import jax.numpy as jnp
from jax import lax
from jax.experimental import pallas as pl
from jax.experimental.pallas import tpu as pltpu
from jax.sharding import PartitionSpec as P

SIDE = 6
LIMIT = 6
SMEM = pl.BlockSpec(memory_space=pltpu.SMEM)
VMEM = pl.BlockSpec(memory_space=pltpu.VMEM)
HBM = pl.BlockSpec(memory_space=pltpu.HBM)
ANY = pl.BlockSpec(memory_space=pl.ANY)


def find_positions(me, position_of, shift, charge, table, plan):
    for i in range(SIDE * SIDE):
        table[i] = -1
    for n in range(charge.shape[1]):
        table[(charge[0, n] + 1) * SIDE + charge[1, n] + 1] = n
    base = (charge[0, me] + 1) * SIDE + charge[1, me] + 1

    def visit(b, carry):
        slot = table[base - shift[0, b] * SIDE - shift[1, b]]
        plan[b] = jnp.where(slot < 0, -1, position_of(me, slot))
        return carry

    lax.fori_loop(0, shift.shape[1], visit, 0)


def list_operators(plan, order, places, skip=0):
    def visit(b, carry):
        count, seen = carry
        position = plan[b]
        index = jnp.int32(-1)
        for i, place in enumerate(places):
            index = jnp.where(position == place, i, index)
        order[0, count] = b
        order[1, count] = index
        here = index >= 0
        if skip:
            here = here & ((position != 0) | (seen >= skip))
            seen = seen + (position == 0).astype(jnp.int32)
        return count + here.astype(jnp.int32), seen

    return lax.fori_loop(0, plan.shape[0], visit, (jnp.int32(0), jnp.int32(0)))[0]


def product(left, source, right):
    halfway, begin = None, 0
    for piece in source:
        end = begin + piece.shape[0]
        term = jnp.dot(left[:, begin:end], piece[...], preferred_element_type=jnp.float32)
        halfway, begin = term if halfway is None else halfway + term, end
    halfway = halfway.astype(jnp.bfloat16)
    return lax.dot_general(halfway, right[...], (((1,), (1,)), ((), ())), preferred_element_type=jnp.float32)


def add_operators(total, count, order, left, right, source, ready):
    def term(i):
        b = order[0, i]
        ready(b)
        return left.at[b], source(order[1, i]), right.at[b]

    def pair(i, carry):
        one, two = term(2 * i), term(2 * i + 1)
        total[...] += product(*one) + product(*two)
        return carry

    lax.fori_loop(0, count // 2, pair, 0)

    @pl.when(count % 2 == 1)
    def _():
        total[...] += product(*term(count - 1))


def each(count, order, act, begin=0):
    def body(i, carry):
        act(order[0, i])
        return carry

    lax.fori_loop(begin, count, body, 0)


class Loads:
    def __init__(self, left_hbm, right_hbm, left, right, sems):
        self.refs = left_hbm, right_hbm, left, right, sems

    def both(self, b, at):
        left_hbm, right_hbm, left, right, sems = self.refs
        return (
            pltpu.make_async_copy(left_hbm.at[b], left.at[at], sems.at[0, at]),
            pltpu.make_async_copy(right_hbm.at[b], right.at[at], sems.at[1, at]),
        )

    def start(self, b, at=None):
        for copy in self.both(b, b if at is None else at):
            copy.start()

    def wait(self, b, at=None):
        for copy in self.both(b, b if at is None else at):
            copy.wait()


def load_sources(pieces, refs, source, sems):
    copies = []
    for i, sizes in enumerate(pieces):
        begin = 0
        for size in sizes:
            at = len(copies)
            copies.append(
                pltpu.make_async_copy(refs[at], source.at[i, pl.ds(begin, size)], sems.at[at])
            )
            begin += size
    for copy in copies:
        copy.start()
    return copies


def first_kernel(position_of, limit, shift_hbm, charge_hbm, left_hbm, right_hbm, own_hbm, *refs):
    total, plan, left, right, source, shift, charge, table, order, sems, small = refs
    copies = [
        pltpu.make_async_copy(shift_hbm, shift, small.at[0]),
        pltpu.make_async_copy(charge_hbm, charge, small.at[1]),
        pltpu.make_async_copy(own_hbm, source.at[0], small.at[2]),
    ]
    for copy in copies:
        copy.start()
    for copy in copies[:2]:
        copy.wait()
    find_positions(lax.axis_index("sec"), position_of, shift, charge, table, plan)
    count = jnp.minimum(list_operators(plan, order, [0]), limit)
    loads = Loads(left_hbm, right_hbm, left, right, sems)

    def start(i, carry):
        loads.start(order[0, i], i)
        order[0, i] = i
        return carry

    lax.fori_loop(0, count, start, 0)
    total[...] = jnp.zeros_like(total)
    copies[2].wait()
    add_operators(
        total, count, order, left, right, lambda at: [source.at[at]], lambda at: loads.wait(0, at)
    )


def second_kernel(pieces, places, skip, others, *refs):
    plan, left_hbm, right_hbm = refs[:3]
    n_in = sum(len(p) for p in pieces)
    inputs, rest = refs[4 : 4 + n_in], refs[4 + n_in :]
    total, left, right, source, now, later, sems, source_sems = rest
    loads = Loads(left_hbm, right_hbm, left, right, sems)
    sources = load_sources(pieces, inputs, source, source_sems)
    count = list_operators(plan, now, places, skip)
    each(count, now, loads.start)
    behind = list_operators(plan, later, others)
    each(behind, later, loads.start)
    for copy in sources:
        copy.wait()
    add_operators(total, count, now, left, right, lambda at: [source.at[at]], loads.wait)
    each(behind, later, loads.wait)


def next_kernel(counts, places, sends, plan, left, right, before, *refs):
    del before
    flat = refs[: sum(counts)]
    total, *outs, order = refs[sum(counts) :]
    begin = 0
    for n, place in zip(counts, places):
        block = flat[begin : begin + n]
        begin += n
        count = list_operators(plan, order, [place])
        add_operators(total, count, order, left, right, lambda at: block, lambda b: None)
    for out, flip in zip(outs, sends):
        rows = out.shape[0]
        at = pl.multiple_of((lax.axis_index("op") ^ flip) * rows, rows)
        out[...] = total[pl.ds(at, rows), :].astype(out.dtype)


def general_kernel(slots, *refs):
    shift, charge, left_hbm, right_hbm, blocks_hbm = refs[:5]
    total, source, left, right, plan, table, order, sems, block_sem = refs[5:]
    copy = pltpu.make_async_copy(blocks_hbm, source, block_sem)
    copy.start()
    find_positions(lax.axis_index("sec"), by_slot, shift, charge, table, plan)
    count = list_operators(plan, order, range(slots))
    loads = Loads(left_hbm, right_hbm, left, right, sems)
    each(count, order, loads.start)
    total[...] = jnp.zeros_like(total)
    copy.wait()
    add_operators(total, count, order, left, right, lambda at: [source.at[at]], loads.wait)


def cost(flops, moved):
    return pl.CostEstimate(flops=flops, bytes_accessed=moved, transcendentals=0)


def in_hbm(x):
    return pltpu.with_memory_space_constraint(x, pltpu.HBM)


def limit_vmem(mib):
    return pltpu.CompilerParams(vmem_limit_bytes=mib << 20)


def start_sum(own, position_of, limit, shift, charge, left_env, right_env):
    operators, rows, inner = left_env.shape
    columns, width = right_env.shape[1:]
    return pl.pallas_call(
        functools.partial(first_kernel, position_of, limit),
        out_shape=[
            jax.ShapeDtypeStruct((rows, columns), jnp.float32),
            jax.ShapeDtypeStruct((operators,), jnp.int32),
        ],
        in_specs=[HBM] * 5,
        out_specs=[VMEM, SMEM],
        scratch_shapes=[
            pltpu.VMEM((limit, rows, inner), jnp.bfloat16),
            pltpu.VMEM((limit, columns, width), jnp.bfloat16),
            pltpu.VMEM((1, inner, width), jnp.bfloat16),
            pltpu.SMEM(shift.shape, jnp.int32),
            pltpu.SMEM(charge.shape, jnp.int32),
            pltpu.SMEM((SIDE * SIDE,), jnp.int32),
            pltpu.SMEM((2, operators + 1), jnp.int32),
            pltpu.SemaphoreType.DMA((2, limit)),
            pltpu.SemaphoreType.DMA((3,)),
        ],
        compiler_params=limit_vmem(24),
        cost_estimate=cost(limit * 4 * rows * inner * width, limit * 4 * rows * inner),
    )(in_hbm(shift), in_hbm(charge), in_hbm(left_env), in_hbm(right_env), in_hbm(own))


def add_and_load(blocks, places, skip, others, plan, left_env, right_env, before):
    pieces = [[p.shape[0] for p in block] for block in blocks]
    flat = [p for block in blocks for p in block]
    operators, rows, inner = left_env.shape
    columns, width = right_env.shape[1:]
    return pl.pallas_call(
        functools.partial(second_kernel, pieces, places, skip, others),
        out_shape=[
            jax.ShapeDtypeStruct(before.shape, jnp.float32),
            jax.ShapeDtypeStruct(left_env.shape, left_env.dtype),
            jax.ShapeDtypeStruct(right_env.shape, right_env.dtype),
        ],
        in_specs=[SMEM, HBM, HBM, VMEM] + [ANY] * len(flat),
        out_specs=[VMEM] * 3,
        input_output_aliases={3: 0},
        scratch_shapes=[
            pltpu.VMEM((len(blocks), inner, width), jnp.bfloat16),
            pltpu.SMEM((2, operators + 1), jnp.int32),
            pltpu.SMEM((2, operators + 1), jnp.int32),
            pltpu.SemaphoreType.DMA((2, operators)),
            pltpu.SemaphoreType.DMA((len(flat),)),
        ],
        compiler_params=limit_vmem(24),
        cost_estimate=cost(operators * 2 * rows * inner * width, operators * 4 * rows * inner),
    )(plan, in_hbm(left_env), in_hbm(right_env), before, *flat)


def add_blocks(blocks, places, sends, ops, plan, left, right, before):
    flat = [p for block in blocks for p in block]
    operators, rows, inner = left.shape
    columns, width = right.shape[1:]
    return pl.pallas_call(
        functools.partial(next_kernel, [len(block) for block in blocks], places, sends),
        out_shape=[jax.ShapeDtypeStruct((rows, columns), jnp.float32)]
        + [
            jax.ShapeDtypeStruct((rows // ops, columns), jnp.bfloat16 if flip else jnp.float32)
            for flip in sends
        ],
        in_specs=[SMEM] + [VMEM] * (3 + len(flat)),
        out_specs=[VMEM] * (1 + len(sends)),
        scratch_shapes=[pltpu.SMEM((2, operators + 1), jnp.int32)],
        input_output_aliases={3: 0},
        compiler_params=limit_vmem(16),
        cost_estimate=cost(operators * rows * inner * width, operators * rows * inner),
    )(plan, left, right, before, *flat)


def sum_all(blocks, shift, charge, left_env, right_env):
    operators, rows, inner = left_env.shape
    columns, width = right_env.shape[1:]
    return pl.pallas_call(
        functools.partial(general_kernel, blocks.shape[0]),
        out_shape=jax.ShapeDtypeStruct((rows, columns), jnp.float32),
        in_specs=[SMEM, SMEM] + [HBM] * 3,
        out_specs=VMEM,
        scratch_shapes=[
            pltpu.VMEM(blocks.shape, blocks.dtype),
            pltpu.VMEM(left_env.shape, left_env.dtype),
            pltpu.VMEM(right_env.shape, right_env.dtype),
            pltpu.SMEM((operators,), jnp.int32),
            pltpu.SMEM((SIDE * SIDE,), jnp.int32),
            pltpu.SMEM((2, operators + 1), jnp.int32),
            pltpu.SemaphoreType.DMA((2, operators)),
            pltpu.SemaphoreType.DMA,
        ],
        compiler_params=limit_vmem(48),
        cost_estimate=cost(operators * 4 * rows * inner * width, operators * 4 * rows * inner),
    )(shift, charge, left_env, right_env, blocks)


def by_slot(me, slot):
    return slot


def by_arrival(me, slot):
    flip = slot ^ me
    turned = ((me ^ lax.axis_index("op")) & 1) == 1
    return jnp.where(turned & (flip >= 2) & (flip < 6), flip ^ 6, flip)


def on_eight(ops, op_shift, sector_charge, own, left_env, right_env):
    secs = 8
    axes = ("op", "sec")
    devices = [(z, s) for z in range(ops) for s in range(secs)]

    def pairs(move):
        return [(z * secs + s, (lambda t: t[0] * secs + t[1])(move(z, s))) for z, s in devices]

    first_flip = lambda z, s: 2 if (z + s) % 2 == 0 else 4
    to_first = pairs(lambda z, s: (z, s ^ first_flip(z, s)))
    to_second = pairs(lambda z, s: (z, s ^ 6 ^ first_flip(z, s)))
    to_core = pairs(lambda z, s: (z, s ^ 1))
    to_plane = pairs(lambda z, s: (z ^ 1, s))
    cut = own.shape[0] // 2
    barrier = lax.optimization_barrier
    later = (3, 4, 6, 7)

    first = lax.ppermute(own, axes, to_first)
    second_bottom = lax.ppermute(own[cut:], axes, to_second)
    other = lax.ppermute(own, axes, to_core)
    total, plan = start_sum(
        own, by_arrival, LIMIT, op_shift.T, sector_charge.T, left_env, right_env
    )
    first, total = barrier((first, total))
    second_top = lax.ppermute(first[:cut], axes, to_plane)
    far = lax.ppermute(first, axes, to_second)
    other_first = lax.ppermute(first, axes, to_core)
    total, left, right = add_and_load(
        [[own], [other], [first], [other_first]], (0, 1, 2, 5), LIMIT, later,
        plan, left_env, right_env, total,
    )
    second_bottom, total = barrier((second_bottom, total))
    other_second_bottom = lax.ppermute(second_bottom, axes, to_core)
    add = functools.partial(add_blocks, ops=ops, plan=plan, left=left, right=right)
    second_top, total = barrier((second_top, total))
    other_second_top = lax.ppermute(second_top, axes, to_core)
    far, total, second_top = barrier((far, total, second_top))
    other_far = lax.ppermute(far, axes, to_core)
    (total,) = add([[second_top, second_bottom], [far]], (4, 6), (), before=total)
    _, *parts = add(
        [[other_second_top, other_second_bottom], [other_far]], (3, 7), tuple(range(ops)),
        before=total,
    )
    result = parts[0]
    for flip in (3, 2, 1):
        sent = lax.ppermute(parts[flip], "op", [(i, i ^ flip) for i in range(ops)])
        result = result + sent.astype(jnp.float32)
    return result


def on_any(secs, ops, op_shift, sector_charge, own, left_env, right_env):
    gathered = lax.all_gather(own, "sec", axis=0)
    total = sum_all(gathered, op_shift.T, sector_charge.T, left_env, right_env)
    rows = total.shape[0] // ops
    me = lax.axis_index("op")
    part = lambda flip: lax.dynamic_slice_in_dim(total, (me ^ flip) * rows, rows, 0)
    result = part(0)
    for flip in range(1, ops):
        sent = part(flip).astype(jnp.bfloat16)
        sent = lax.ppermute(sent, "op", [(i, i ^ flip) for i in range(ops)])
        result = result + sent.astype(jnp.float32)
    return result


def on_device(secs, ops, state_vector, left_env, right_env, op_shift, sector_charge):
    own = state_vector.reshape(state_vector.shape[0], state_vector.shape[2])
    left_env = left_env.reshape(left_env.shape[0], *left_env.shape[2:])
    right_env = right_env.reshape(right_env.shape[0], *right_env.shape[2:])
    apply = (
        functools.partial(on_eight, ops)
        if secs == 8 and ops == 4
        else functools.partial(on_any, secs, ops)
    )
    hpsi = apply(op_shift, sector_charge, own, left_env, right_env)
    return hpsi.astype(jnp.bfloat16)[:, None, :]


def solution(mesh):
    placed = (
        P(None, "sec", None),
        P("op", "sec", None, None),
        P("op", "sec", None, None),
        P("op", None),
        P(),
    )
    return jax.shard_map(
        functools.partial(on_device, mesh.shape["sec"], mesh.shape["op"]),
        mesh=mesh,
        in_specs=placed,
        out_specs=P("op", "sec", None),
        check_vma=False,
    )
```

```python
import functools

import jax
import jax.numpy as jnp
from jax import lax
from jax.experimental import pallas as pl
from jax.experimental.pallas import tpu as pltpu
from jax.sharding import PartitionSpec as P

SIDE = 6
LIMIT = 6
SMEM = pl.BlockSpec(memory_space=pltpu.SMEM)
VMEM = pl.BlockSpec(memory_space=pltpu.VMEM)
HBM = pl.BlockSpec(memory_space=pltpu.HBM)
ANY = pl.BlockSpec(memory_space=pl.ANY)


def find_positions(me, position_of, shift, charge, table, plan):
    for i in range(SIDE * SIDE):
        table[i] = -1
    for n in range(charge.shape[1]):
        table[(charge[0, n] + 1) * SIDE + charge[1, n] + 1] = n
    base = (charge[0, me] + 1) * SIDE + charge[1, me] + 1

    def visit(b, carry):
        slot = table[base - shift[0, b] * SIDE - shift[1, b]]
        plan[b] = jnp.where(slot < 0, -1, position_of(me, slot))
        return carry

    lax.fori_loop(0, shift.shape[1], visit, 0)


def list_operators(plan, order, places, skip=0):
    def visit(b, carry):
        count, seen = carry
        position = plan[b]
        index = jnp.int32(-1)
        for i, place in enumerate(places):
            index = jnp.where(position == place, i, index)
        order[0, count] = b
        order[1, count] = index
        here = index >= 0
        if skip:
            here = here & ((position != 0) | (seen >= skip))
            seen = seen + (position == 0).astype(jnp.int32)
        return count + here.astype(jnp.int32), seen

    return lax.fori_loop(0, plan.shape[0], visit, (jnp.int32(0), jnp.int32(0)))[0]


def product(left, source, right):
    halfway, begin = None, 0
    for piece in source:
        end = begin + piece.shape[0]
        term = jnp.dot(left[:, begin:end], piece[...], preferred_element_type=jnp.float32)
        halfway, begin = term if halfway is None else halfway + term, end
    halfway = halfway.astype(jnp.bfloat16)
    return lax.dot_general(halfway, right[...], (((1,), (1,)), ((), ())), preferred_element_type=jnp.float32)


def sort_operators(plan, orders):
    for place in range(orders.shape[0]):
        orders[place, 0] = 0

    def visit(b, carry):
        place = jnp.maximum(plan[b], 0)
        count = orders[place, 0] + 1
        orders[place, count] = b
        orders[place, 0] = jnp.where(plan[b] < 0, count - 1, count)
        return carry

    lax.fori_loop(0, plan.shape[0], visit, 0)


def add_operators(total, count, pick, left, right, ready):
    def term(i):
        b, source = pick(i)
        ready(b)
        return left.at[b], source, right.at[b]

    def pair(i, carry):
        one, two = term(2 * i), term(2 * i + 1)
        total[...] += product(*one) + product(*two)
        return carry

    lax.fori_loop(0, count // 2, pair, 0)

    @pl.when(count % 2 == 1)
    def _():
        total[...] += product(*term(count - 1))


def each(count, order, act, begin=0):
    def body(i, carry):
        act(order[0, i])
        return carry

    lax.fori_loop(begin, count, body, 0)


class Loads:
    def __init__(self, left_hbm, right_hbm, left, right, sems):
        self.refs = left_hbm, right_hbm, left, right, sems

    def both(self, b, at):
        left_hbm, right_hbm, left, right, sems = self.refs
        return (
            pltpu.make_async_copy(left_hbm.at[b], left.at[at], sems.at[0, at]),
            pltpu.make_async_copy(right_hbm.at[b], right.at[at], sems.at[1, at]),
        )

    def start(self, b, at=None):
        for copy in self.both(b, b if at is None else at):
            copy.start()

    def wait(self, b, at=None):
        for copy in self.both(b, b if at is None else at):
            copy.wait()


def load_sources(pieces, refs, source, sems):
    copies = []
    for i, sizes in enumerate(pieces):
        begin = 0
        for size in sizes:
            at = len(copies)
            copies.append(
                pltpu.make_async_copy(refs[at], source.at[i, pl.ds(begin, size)], sems.at[at])
            )
            begin += size
    for copy in copies:
        copy.start()
    return copies


def first_kernel(position_of, limit, shift_hbm, charge_hbm, left_hbm, right_hbm, own_hbm, *refs):
    total, plan, left, right, source, shift, charge, table, order, sems, small = refs
    copies = [
        pltpu.make_async_copy(shift_hbm, shift, small.at[0]),
        pltpu.make_async_copy(charge_hbm, charge, small.at[1]),
        pltpu.make_async_copy(own_hbm, source.at[0], small.at[2]),
    ]
    for copy in copies:
        copy.start()
    for copy in copies[:2]:
        copy.wait()
    find_positions(lax.axis_index("sec"), position_of, shift, charge, table, plan)
    count = jnp.minimum(list_operators(plan, order, [0]), limit)
    loads = Loads(left_hbm, right_hbm, left, right, sems)

    def start(i, carry):
        loads.start(order[0, i], i)
        return carry

    lax.fori_loop(0, count, start, 0)
    total[...] = jnp.zeros_like(total)
    copies[2].wait()
    add_operators(
        total, count, lambda i: (i, [source.at[0]]), left, right, lambda at: loads.wait(0, at)
    )


def second_kernel(pieces, places, skip, others, *refs):
    plan, left_hbm, right_hbm = refs[:3]
    n_in = sum(len(p) for p in pieces)
    inputs, rest = refs[4 : 4 + n_in], refs[4 + n_in :]
    total, orders, left, right, source, now, later, sems, source_sems = rest
    loads = Loads(left_hbm, right_hbm, left, right, sems)
    sources = load_sources(pieces, inputs, source, source_sems)
    count = list_operators(plan, now, places, skip)
    each(count, now, loads.start)
    behind = list_operators(plan, later, others)
    each(behind, later, loads.start)
    sort_operators(plan, orders)
    for copy in sources:
        copy.wait()
    add_operators(
        total, count, lambda i: (now[0, i], [source.at[now[1, i]]]), left, right, loads.wait
    )
    each(behind, later, loads.wait)


def next_kernel(counts, places, sends, orders, left, right, before, *refs):
    del before
    flat, (total, *outs) = refs[: sum(counts)], refs[sum(counts) :]
    begin = 0
    for n, place in zip(counts, places):
        block = flat[begin : begin + n]
        begin += n
        add_operators(
            total, orders[place, 0], lambda i: (orders[place, i + 1], block), left, right, lambda b: None
        )
    for out, flip in zip(outs, sends):
        rows = out.shape[0]
        at = pl.multiple_of((lax.axis_index("op") ^ flip) * rows, rows)
        out[...] = total[pl.ds(at, rows), :].astype(out.dtype)


def general_kernel(slots, *refs):
    shift, charge, left_hbm, right_hbm, blocks_hbm = refs[:5]
    total, source, left, right, plan, table, order, sems, block_sem = refs[5:]
    copy = pltpu.make_async_copy(blocks_hbm, source, block_sem)
    copy.start()
    find_positions(lax.axis_index("sec"), by_slot, shift, charge, table, plan)
    count = list_operators(plan, order, range(slots))
    loads = Loads(left_hbm, right_hbm, left, right, sems)
    each(count, order, loads.start)
    total[...] = jnp.zeros_like(total)
    copy.wait()
    add_operators(
        total, count, lambda i: (order[0, i], [source.at[order[1, i]]]), left, right, loads.wait
    )


def cost(flops, moved):
    return pl.CostEstimate(flops=flops, bytes_accessed=moved, transcendentals=0)


def in_hbm(x):
    return pltpu.with_memory_space_constraint(x, pltpu.HBM)


def limit_vmem(mib):
    return pltpu.CompilerParams(vmem_limit_bytes=mib << 20)


def start_sum(own, position_of, limit, shift, charge, left_env, right_env):
    operators, rows, inner = left_env.shape
    columns, width = right_env.shape[1:]
    return pl.pallas_call(
        functools.partial(first_kernel, position_of, limit),
        out_shape=[
            jax.ShapeDtypeStruct((rows, columns), jnp.float32),
            jax.ShapeDtypeStruct((operators,), jnp.int32),
        ],
        in_specs=[HBM] * 5,
        out_specs=[VMEM, SMEM],
        scratch_shapes=[
            pltpu.VMEM((limit, rows, inner), jnp.bfloat16),
            pltpu.VMEM((limit, columns, width), jnp.bfloat16),
            pltpu.VMEM((1, inner, width), jnp.bfloat16),
            pltpu.SMEM(shift.shape, jnp.int32),
            pltpu.SMEM(charge.shape, jnp.int32),
            pltpu.SMEM((SIDE * SIDE,), jnp.int32),
            pltpu.SMEM((2, operators + 1), jnp.int32),
            pltpu.SemaphoreType.DMA((2, limit)),
            pltpu.SemaphoreType.DMA((3,)),
        ],
        compiler_params=limit_vmem(24),
        cost_estimate=cost(limit * 4 * rows * inner * width, limit * 4 * rows * inner),
    )(in_hbm(shift), in_hbm(charge), in_hbm(left_env), in_hbm(right_env), in_hbm(own))


def add_and_load(blocks, places, skip, others, plan, left_env, right_env, before):
    pieces = [[p.shape[0] for p in block] for block in blocks]
    flat = [p for block in blocks for p in block]
    operators, rows, inner = left_env.shape
    columns, width = right_env.shape[1:]
    return pl.pallas_call(
        functools.partial(second_kernel, pieces, places, skip, others),
        out_shape=[
            jax.ShapeDtypeStruct(before.shape, jnp.float32),
            jax.ShapeDtypeStruct((8, operators + 2), jnp.int32),
            jax.ShapeDtypeStruct(left_env.shape, left_env.dtype),
            jax.ShapeDtypeStruct(right_env.shape, right_env.dtype),
        ],
        in_specs=[SMEM, HBM, HBM, VMEM] + [ANY] * len(flat),
        out_specs=[VMEM, SMEM, VMEM, VMEM],
        input_output_aliases={3: 0},
        scratch_shapes=[
            pltpu.VMEM((len(blocks), inner, width), jnp.bfloat16),
            pltpu.SMEM((2, operators + 1), jnp.int32),
            pltpu.SMEM((2, operators + 1), jnp.int32),
            pltpu.SemaphoreType.DMA((2, operators)),
            pltpu.SemaphoreType.DMA((len(flat),)),
        ],
        compiler_params=limit_vmem(24),
        cost_estimate=cost(operators * 2 * rows * inner * width, operators * 4 * rows * inner),
    )(plan, in_hbm(left_env), in_hbm(right_env), before, *flat)


def add_blocks(blocks, places, sends, ops, orders, left, right, before):
    flat = [p for block in blocks for p in block]
    operators, rows, inner = left.shape
    columns, width = right.shape[1:]
    return pl.pallas_call(
        functools.partial(next_kernel, [len(block) for block in blocks], places, sends),
        out_shape=[jax.ShapeDtypeStruct((rows, columns), jnp.float32)]
        + [
            jax.ShapeDtypeStruct((rows // ops, columns), jnp.bfloat16 if flip else jnp.float32)
            for flip in sends
        ],
        in_specs=[SMEM] + [VMEM] * (3 + len(flat)),
        out_specs=[VMEM] * (1 + len(sends)),
        input_output_aliases={3: 0},
        compiler_params=limit_vmem(16),
        cost_estimate=cost(operators * rows * inner * width, operators * rows * inner),
    )(orders, left, right, before, *flat)


def sum_all(blocks, shift, charge, left_env, right_env):
    operators, rows, inner = left_env.shape
    columns, width = right_env.shape[1:]
    return pl.pallas_call(
        functools.partial(general_kernel, blocks.shape[0]),
        out_shape=jax.ShapeDtypeStruct((rows, columns), jnp.float32),
        in_specs=[SMEM, SMEM] + [HBM] * 3,
        out_specs=VMEM,
        scratch_shapes=[
            pltpu.VMEM(blocks.shape, blocks.dtype),
            pltpu.VMEM(left_env.shape, left_env.dtype),
            pltpu.VMEM(right_env.shape, right_env.dtype),
            pltpu.SMEM((operators,), jnp.int32),
            pltpu.SMEM((SIDE * SIDE,), jnp.int32),
            pltpu.SMEM((2, operators + 1), jnp.int32),
            pltpu.SemaphoreType.DMA((2, operators)),
            pltpu.SemaphoreType.DMA,
        ],
        compiler_params=limit_vmem(48),
        cost_estimate=cost(operators * 4 * rows * inner * width, operators * 4 * rows * inner),
    )(shift, charge, left_env, right_env, blocks)


def by_slot(me, slot):
    return slot


def by_arrival(me, slot):
    flip = slot ^ me
    turned = ((me ^ lax.axis_index("op")) & 1) == 1
    return jnp.where(turned & (flip >= 2) & (flip < 6), flip ^ 6, flip)


def on_eight(ops, op_shift, sector_charge, own, left_env, right_env):
    secs = 8
    axes = ("op", "sec")
    devices = [(z, s) for z in range(ops) for s in range(secs)]

    def pairs(move):
        return [(z * secs + s, (lambda t: t[0] * secs + t[1])(move(z, s))) for z, s in devices]

    first_flip = lambda z, s: 2 if (z + s) % 2 == 0 else 4
    to_first = pairs(lambda z, s: (z, s ^ first_flip(z, s)))
    to_second = pairs(lambda z, s: (z, s ^ 6 ^ first_flip(z, s)))
    to_core = pairs(lambda z, s: (z, s ^ 1))
    to_plane = pairs(lambda z, s: (z ^ 1, s))
    cut = own.shape[0] // 2
    barrier = lax.optimization_barrier
    later = (3, 4, 6, 7)

    first = lax.ppermute(own, axes, to_first)
    second_bottom = lax.ppermute(own[cut:], axes, to_second)
    other = lax.ppermute(own, axes, to_core)
    total, plan = start_sum(
        own, by_arrival, LIMIT, op_shift.T, sector_charge.T, left_env, right_env
    )
    first, total = barrier((first, total))
    second_top = lax.ppermute(first[:cut], axes, to_plane)
    far = lax.ppermute(first, axes, to_second)
    other_first = lax.ppermute(first, axes, to_core)
    total, orders, left, right = add_and_load(
        [[own], [other], [first], [other_first]], (0, 1, 2, 5), LIMIT, later,
        plan, left_env, right_env, total,
    )
    second_bottom, total = barrier((second_bottom, total))
    other_second_bottom = lax.ppermute(second_bottom, axes, to_core)
    add = functools.partial(add_blocks, ops=ops, orders=orders, left=left, right=right)
    second_top, total = barrier((second_top, total))
    other_second_top = lax.ppermute(second_top, axes, to_core)
    far, total, second_top = barrier((far, total, second_top))
    other_far = lax.ppermute(far, axes, to_core)
    (total,) = add([[second_top, second_bottom], [far]], (4, 6), (), before=total)
    _, *parts = add(
        [[other_second_top, other_second_bottom], [other_far]], (3, 7), tuple(range(ops)),
        before=total,
    )
    result = parts[0]
    for flip in (3, 2, 1):
        sent = lax.ppermute(parts[flip], "op", [(i, i ^ flip) for i in range(ops)])
        result = result + sent.astype(jnp.float32)
    return result


def on_any(secs, ops, op_shift, sector_charge, own, left_env, right_env):
    gathered = lax.all_gather(own, "sec", axis=0)
    total = sum_all(gathered, op_shift.T, sector_charge.T, left_env, right_env)
    rows = total.shape[0] // ops
    me = lax.axis_index("op")
    part = lambda flip: lax.dynamic_slice_in_dim(total, (me ^ flip) * rows, rows, 0)
    result = part(0)
    for flip in range(1, ops):
        sent = part(flip).astype(jnp.bfloat16)
        sent = lax.ppermute(sent, "op", [(i, i ^ flip) for i in range(ops)])
        result = result + sent.astype(jnp.float32)
    return result


def on_device(secs, ops, state_vector, left_env, right_env, op_shift, sector_charge):
    own = state_vector.reshape(state_vector.shape[0], state_vector.shape[2])
    left_env = left_env.reshape(left_env.shape[0], *left_env.shape[2:])
    right_env = right_env.reshape(right_env.shape[0], *right_env.shape[2:])
    apply = (
        functools.partial(on_eight, ops)
        if secs == 8 and ops == 4
        else functools.partial(on_any, secs, ops)
    )
    hpsi = apply(op_shift, sector_charge, own, left_env, right_env)
    return hpsi.astype(jnp.bfloat16)[:, None, :]


def solution(mesh):
    placed = (
        P(None, "sec", None),
        P("op", "sec", None, None),
        P("op", "sec", None, None),
        P("op", None),
        P(),
    )
    return jax.shard_map(
        functools.partial(on_device, mesh.shape["sec"], mesh.shape["op"]),
        mesh=mesh,
        in_specs=placed,
        out_specs=P("op", "sec", None),
        check_vma=False,
    )
```
